32 devices in a mesh: section: 2 (over core), seq: 4 (over z), fsdp: 4 (over y, x).
Axes of the slice: x: 2, y: 2, z: 4, core: 2. Of those that a mesh axis runs over, the one named last changes fastest.
Arguments:
- inputs: bfloat16 [2, 8, 1024, 1024], P(None, 'fsdp', 'seq'), may hold values from -6 to 6
- cotangent: bfloat16 [2, 8, 1024, 1024], P(None, 'fsdp', 'seq'), may hold values from -6 to 6
- ln1_gain: bfloat16 [2, 1024], P('section', 'fsdp'), may hold values from 0.5 to 1.5
- ln1_bias: bfloat16 [2, 1024], P('section', 'fsdp'), may hold values from -3 to 3
- ln2_gain: bfloat16 [2, 1024], P('section', 'fsdp'), may hold values from 0.5 to 1.5
- ln2_bias: bfloat16 [2, 1024], P('section', 'fsdp'), may hold values from -3 to 3
- w_qkv: bfloat16 [2, 1024, 3072], P('section', 'fsdp'), may hold values from -5 to 5
- w_out: bfloat16 [2, 1024, 1024], P('section', 'fsdp'), may hold values from -1.5 to 1.5
- w_up: bfloat16 [2, 1024, 4096], P('section', 'fsdp'), may hold values from -0.1875 to 0.1875
- w_down: bfloat16 [2, 4096, 1024], P('section', 'fsdp'), may hold values from -0.09375 to 0.09375
Outputs:
- section_outputs: bfloat16 [2, 2, 8, 1024, 1024], P('section', None, 'fsdp', 'seq')
- section_input_grads: bfloat16 [2, 2, 8, 1024, 1024], P('section', None, 'fsdp', 'seq')
- grad_ln1_gain: float32 [2, 1024], P('section', 'fsdp')
- grad_ln1_bias: float32 [2, 1024], P('section', 'fsdp')
- grad_ln2_gain: float32 [2, 1024], P('section', 'fsdp')
- grad_ln2_bias: float32 [2, 1024], P('section', 'fsdp')
- grad_w_qkv: float32 [2, 1024, 3072], P('section', 'fsdp')
- grad_w_out: float32 [2, 1024, 1024], P('section', 'fsdp')
- grad_w_up: float32 [2, 1024, 4096], P('section', 'fsdp')
- grad_w_down: float32 [2, 4096, 1024], P('section', 'fsdp')
The draws below stay inside these ranges and needn't reach their ends.
All inputs are finite; a program needn't handle non-finite values.
Results may differ from the reference program's by a relative error of at most 0.017.
Values may be sent and summed in bfloat16 or wider, within the bound.
No kernel may reach another device: no remote copies, remote signals or barrier semaphores. Data moves between devices by JAX's collectives and lax.ppermute only.
A program may use at most 384 MiB of HBM per device.

```python
import math
import jax
import jax.numpy as jnp
from jax import lax

D = 1024
H = 16
HD = 64
ROT = 16
FF = 4096
M = 2
LEN = 1024
SEQS = 8
N_SECTION = 2


def draw_w_qkv(key, part):
    key_base = jax.random.fold_in(key, 11)
    key_rank = jax.random.fold_in(key, 12)
    key_level = jax.random.fold_in(key, 13)
    base = jax.random.truncated_normal(key_base, -6.0, 6.0, (2, D, 3 * D), jnp.float32)
    level = jnp.exp(jax.random.uniform(key_level, (2, H), jnp.float32, 0.1, 0.5))
    order = jax.vmap(lambda one: jax.random.permutation(one, H))(jax.random.split(key_rank, 2))
    head_level = jnp.where(order < 3, level, jnp.float32(1.0))
    column = jnp.repeat(head_level, HD, axis=1)
    column_scale = jnp.concatenate([column, column, jnp.ones((2, D), jnp.float32)], axis=1)
    return (base * float(D) ** (-0.5) * column_scale[:, None, :]).astype(jnp.bfloat16)


def shard_levels(own_key, extent, shards, least, top_value):
    def one(axis_at, blocks):
        heights = jax.random.uniform(jax.random.fold_in(jax.random.fold_in(own_key, 6), axis_at), (blocks,), jnp.float32, least / len(shards), top_value / len(shards))
        return jnp.repeat(jnp.exp(heights), extent[axis_at] // blocks).reshape((-1,) + (1,) * (len(extent) - axis_at - 1))

    loudness = one(*shards[0])
    for cut in shards[1:]:
        loudness = loudness * one(*cut)
    return loudness


def gaussian(key, extent, scale, most, shards=(), kind=jnp.bfloat16):
    result = jax.random.normal(key, extent, jnp.float32) * scale
    if len(shards) > 0:
        result = shard_levels(key, extent, shards, -0.22, 0.18) * result
    return jnp.clip(result, min=-most, max=most).astype(kind)


def setup_inputs(seed: int = 0) -> dict:
    streams_of = jax.random.split(jax.random.key(seed), 11)
    return {
        "inputs": gaussian(streams_of[0], (M, SEQS, LEN, D), 1.0, 6.0, ((1, 4), (2, 4))),
        "cotangent": gaussian(streams_of[1], (M, SEQS, LEN, D), 1.0, 6.0, ((1, 4), (2, 4))),
        "ln1_gain": jnp.clip(1.0 + 0.1 * jax.random.normal(streams_of[2], (N_SECTION, D), jnp.float32), 0.5, 1.5).astype(jnp.bfloat16),
        "ln1_bias": gaussian(streams_of[3], (N_SECTION, D), 0.5, 3.0, ((0, 2), (1, 4))),
        "ln2_gain": jnp.clip(1.0 + 0.1 * jax.random.normal(streams_of[4], (N_SECTION, D), jnp.float32), 0.5, 1.5).astype(jnp.bfloat16),
        "ln2_bias": gaussian(streams_of[5], (N_SECTION, D), 0.5, 3.0, ((0, 2), (1, 4))),
        "w_qkv": draw_w_qkv(jax.random.fold_in(streams_of[10], 71), 0),
        "w_out": gaussian(streams_of[7], (N_SECTION, D, D), (D // 64) ** -0.5, 1.5, ((0, 2), (1, 4))),
        "w_up": gaussian(streams_of[8], (N_SECTION, D, FF), D ** -0.5, 0.1875, ((0, 2), (1, 4))),
        "w_down": gaussian(streams_of[9], (N_SECTION, FF, D), FF ** -0.5, 0.09375, ((0, 2), (1, 4))),
    }


@jax.custom_vjp
def low(v):
    return lax.optimization_barrier(v.astype(jnp.bfloat16)).astype(jnp.float32)

@jax.custom_vjp
def low_back(v):
    return v

def low_keep(v):
    return (low(v), None)

def low_pass(kept, grad):
    return (grad,)

def back_keep(v):
    return (v, None)

def back_low(kept, grad):
    return (low(grad),)
low.defvjp(low_keep, low_pass)
low_back.defvjp(back_keep, back_low)
eps_norm = 1e-05
rope_base = 10000.0
HIGH = lax.Precision.HIGHEST

def normalize(xval, gain, shift):
    mean = lax.optimization_barrier(jnp.mean(xval, axis=-1, keepdims=True))
    cent = xval - mean
    scale = lax.rsqrt(lax.optimization_barrier(jnp.mean(cent * cent, axis=-1, keepdims=True)) + eps_norm)
    return cent * scale * gain + shift

def rotary_tables(positions):
    freqs = jnp.power(rope_base, -jnp.arange(0, ROT, 2).astype(jnp.float32) / ROT)
    angles = positions[:, None] * freqs[None, :]
    return (jnp.cos(angles), jnp.sin(angles))

def rotate(block, cosine, sine, sign):
    half = ROT // 2
    first = block[..., :half]
    second = block[..., half:ROT]
    cos_b = cosine[:, None, :]
    sin_b = sine[:, None, :] * sign
    return jnp.concatenate([first * cos_b - second * sin_b, second * cos_b + first * sin_b, block[..., ROT:]], axis=-1)

def head_attention(query, key, value):
    length = query.shape[0]
    scores = low_back(jnp.dot(query, key.T, precision=HIGH) * (1.0 / math.sqrt(HD)))
    places = jnp.arange(length)
    scores = jnp.where(places[None, :] <= places[:, None], scores, -jnp.inf)
    top = lax.optimization_barrier(jnp.max(scores, axis=-1, keepdims=True))
    expd = jnp.exp(scores - top)
    probs = expd / lax.optimization_barrier(jnp.sum(expd, axis=-1, keepdims=True))
    return jnp.dot(low(probs), value, precision=HIGH)

def layer(xval, gain_one, bias_one, gain_two, bias_two, w_qkv, w_out, w_up, w_down):
    batch, length, width = xval.shape
    normed_a = low(normalize(xval, gain_one, bias_one))
    normed_c = low(normalize(xval, gain_two, bias_two))
    mixed = low_back(jnp.einsum('bld,de->ble', normed_a, w_qkv, precision=HIGH)).reshape(batch, length, 3, H, HD)
    cosine, sine = rotary_tables(jnp.arange(length).astype(jnp.float32))
    query = low(low_back(rotate(mixed[:, :, 0], cosine, sine, 1.0)))
    key = low(low_back(rotate(mixed[:, :, 1], cosine, sine, 1.0)))
    value = low(low_back(mixed[:, :, 2]))

    def flatten(arr):
        return arr.transpose(0, 2, 1, 3).reshape(batch * H, length, HD)
    outs = lax.map(lambda trio: jax.checkpoint(head_attention)(trio[0], trio[1], trio[2]), (flatten(query), flatten(key), flatten(value)))
    attended = outs.reshape(batch, H, length, HD).transpose(0, 2, 1, 3).reshape(batch, length, width)
    attended = low(low_back(attended))
    attn = low_back(jnp.einsum('bld,de->ble', attended, w_out, precision=HIGH))
    pre = low_back(jnp.einsum('bld,df->blf', normed_c, w_up, precision=HIGH))
    hidden = low(jax.nn.gelu(pre, approximate=False))
    mlp = low_back(jnp.einsum('blf,fd->bld', hidden, w_down, precision=HIGH))
    return xval + attn + mlp

def reference(inputs, cotangent, ln1_gain, ln1_bias, ln2_gain, ln2_bias, w_qkv, w_out, w_up, w_down):
    micro, seqs, length, width = inputs.shape
    xval = inputs.astype(jnp.float32).reshape(micro * seqs, length, width)
    cot = cotangent.astype(jnp.float32).reshape(micro * seqs, length, width)
    weights = tuple((w.astype(jnp.float32) for w in (ln1_gain, ln1_bias, ln2_gain, ln2_bias, w_qkv, w_out, w_up, w_down)))
    spare = jnp.zeros_like(xval)

    def forward(xin, extra, g1, b1, g2, b2, wq, wo, wu, wd):
        first = low(low_back(layer(xin, g1[0], b1[0], g2[0], b2[0], wq[0], wo[0], wu[0], wd[0]))) + extra
        second = layer(first, g1[1], b1[1], g2[1], b2[1], wq[1], wo[1], wu[1], wd[1])
        return (second, first)
    final, pullback, middle = jax.vjp(forward, xval, spare, *weights, has_aux=True)
    grads = pullback(cot)
    shape = (micro, seqs, length, width)
    outputs = jnp.stack([middle.reshape(shape), final.reshape(shape)]).astype(jnp.bfloat16)
    input_grads = jnp.stack([grads[0].reshape(shape), grads[1].reshape(shape)]).astype(jnp.bfloat16)
    return (outputs, input_grads, grads[2], grads[3], grads[4], grads[5], grads[6], grads[7], grads[8], grads[9])
```

```python
import functools
import math

import jax
import jax.numpy as jnp
from jax import lax
from jax.experimental import pallas as pl
from jax.experimental.pallas import tpu as pltpu
from jax.sharding import PartitionSpec as P

H = 16
HD = 64
ROT = 16


eps_norm = 1e-05
rope_base = 10000.0
bfloat = jnp.bfloat16
single = jnp.float32


def as_sent(value):
    return jax.tree.map(lambda a: a.astype(jnp.bfloat16) if a.dtype == jnp.float32 else a, value)


def from_behind(block, axis, distance):
    devices = range(lax.axis_size(axis))
    route = [(i - distance, i) for i in devices if i - distance in devices]
    return lax.ppermute(block, axis, route)


def normalize(xval, gain, shift):
    mean = jnp.mean(xval, axis=-1, keepdims=True)
    cent = xval - mean
    scale = lax.rsqrt(jnp.mean(cent * cent, axis=-1, keepdims=True) + eps_norm)
    unit = cent * scale
    return (unit * gain + shift, unit, scale)


def norm_back(grad, unit, scale, gain):
    dunit = grad * gain
    inner = (
        dunit
        - jnp.mean(dunit, axis=-1, keepdims=True)
        - unit * jnp.mean(dunit * unit, axis=-1, keepdims=True)
    )
    return (scale * inner, jnp.sum(grad * unit, axis=0), jnp.sum(grad, axis=0))


def rotary_tables(positions):
    freqs = jnp.power(rope_base, -jnp.arange(0, ROT, 2).astype(single) / ROT)
    angles = positions[:, None] * freqs[None, :]
    return (jnp.cos(angles), jnp.sin(angles))


def rotate(block, cosine, sine, sign):
    half = ROT // 2
    first = block[..., :half]
    second = block[..., half:ROT]
    cos_b = cosine[:, None, :]
    sin_b = sine[:, None, :] * sign
    return jnp.concatenate(
        [first * cos_b - second * sin_b, second * cos_b + first * sin_b, block[..., ROT:]], axis=-1
    )


def gelu_slope(value):
    return 0.5 * (1.0 + lax.erf(value * (1.0 / math.sqrt(2.0)))) + value * jnp.exp(
        -0.5 * value * value
    ) * (1.0 / math.sqrt(2.0 * math.pi))


def block_scores(query_blk, key_heads, start):
    block = query_blk.shape[1]
    length = key_heads.shape[1]
    scores = jnp.einsum("sqhd,skhd->shqk", query_blk, key_heads, preferred_element_type=single) * (
        1.0 / math.sqrt(HD)
    )
    query_pos = start + jnp.arange(block)
    key_pos = jnp.arange(length)
    return jnp.where(key_pos[None, :] <= query_pos[:, None], scores, -jnp.inf)


def attend(query_heads, key_heads, value_heads, block):
    seqs, length, local, size = query_heads.shape
    count = length // block

    def one_block(start):
        query_blk = lax.dynamic_slice_in_dim(query_heads, start, block, 1)
        scores = block_scores(query_blk, key_heads, start)
        top = jnp.max(scores, axis=-1, keepdims=True)
        expd = jnp.exp(scores - top)
        total = jnp.sum(expd, axis=-1, keepdims=True)
        probs = (expd / total).astype(bfloat)
        out = jnp.einsum("shqk,skhd->sqhd", probs, value_heads, preferred_element_type=single)
        return (out.astype(bfloat), top[..., 0] + jnp.log(total[..., 0]))

    outs, logsum = lax.map(one_block, jnp.arange(count) * block)
    outs = outs.transpose(1, 0, 2, 3, 4).reshape(seqs, length, local, size)
    return (outs, logsum)


def attend_back(query_heads, key_heads, value_heads, grad_out, logsum, block):
    seqs, length, local, size = query_heads.shape
    count = length // block
    scale = 1.0 / math.sqrt(size)

    def step(carry, item):
        grad_key, grad_value = carry
        start, logsum_blk = item
        query_blk = lax.dynamic_slice_in_dim(query_heads, start, block, 1)
        grad_blk = lax.dynamic_slice_in_dim(grad_out, start, block, 1)
        scores = block_scores(query_blk, key_heads, start)
        probs = jnp.exp(scores - logsum_blk[..., None])
        grad_probs = jnp.einsum(
            "sqhd,skhd->shqk", grad_blk, value_heads, preferred_element_type=single
        )
        delta = jnp.sum(probs * grad_probs, axis=-1, keepdims=True)
        grad_scores = (probs * (grad_probs - delta)).astype(bfloat)
        grad_query = (
            jnp.einsum("shqk,skhd->sqhd", grad_scores, key_heads, preferred_element_type=single)
            * scale
        )
        grad_key = (
            grad_key
            + jnp.einsum("shqk,sqhd->skhd", grad_scores, query_blk, preferred_element_type=single)
            * scale
        )
        grad_value = grad_value + jnp.einsum(
            "shqk,sqhd->skhd", probs.astype(bfloat), grad_blk, preferred_element_type=single
        )
        return ((grad_key, grad_value), grad_query)

    zeros = jnp.zeros((seqs, length, local, size), single)
    (grad_key, grad_value), grad_query = lax.scan(
        step, (zeros, zeros), (jnp.arange(count) * block, logsum)
    )
    grad_query = grad_query.transpose(1, 0, 2, 3, 4).reshape(seqs, length, local, size)
    return (grad_query, grad_key, grad_value)


def forward_layer(feed, params, cosine, sine):
    gain_one, bias_one, gain_two, bias_two, w_qkv, w_out, w_up, w_down = params
    seqs, toks, width = feed.shape
    flat = feed.astype(single).reshape(seqs * toks, width)
    normed_a, _, _ = normalize(flat, gain_one.astype(single), bias_one.astype(single))
    normed_c, _, _ = normalize(flat, gain_two.astype(single), bias_two.astype(single))
    mixed = jnp.dot(normed_a.astype(bfloat), w_qkv, preferred_element_type=single).reshape(
        seqs, toks, 3, H, HD
    )
    query = rotate(mixed[:, :, 0], cosine, sine, 1.0).astype(bfloat).reshape(seqs, toks, width)
    key = rotate(mixed[:, :, 1], cosine, sine, 1.0).astype(bfloat).reshape(seqs, toks, width)
    value = mixed[:, :, 2].astype(bfloat).reshape(seqs, toks, width)
    query_heads, key_heads, value_heads = (
        lax.all_to_all(query, "seq", split_axis=2, concat_axis=1, tiled=True),
        lax.all_to_all(key, "seq", split_axis=2, concat_axis=1, tiled=True),
        lax.all_to_all(value, "seq", split_axis=2, concat_axis=1, tiled=True),
    )
    length = query_heads.shape[1]
    local = query_heads.shape[2] // HD
    shape_heads = (seqs, length, local, HD)
    query_heads = query_heads.reshape(shape_heads)
    key_heads = key_heads.reshape(shape_heads)
    value_heads = value_heads.reshape(shape_heads)
    block = min(512, length)
    attended, logsum = attend(query_heads, key_heads, value_heads, block)
    merged = lax.all_to_all(
        attended.reshape(seqs, length, local * HD), "seq", split_axis=1, concat_axis=2, tiled=True
    )
    merged = merged.reshape(seqs * toks, width)
    attn = jnp.dot(merged, w_out, preferred_element_type=single)
    hidden_pre = jnp.dot(normed_c.astype(bfloat), w_up, preferred_element_type=single)
    hidden = jax.nn.gelu(hidden_pre, approximate=False).astype(bfloat)
    mlp = jnp.dot(hidden, w_down, preferred_element_type=single)
    result = (flat + attn + mlp).reshape(seqs, toks, width)
    kept = (feed, query_heads, key_heads, value_heads, attended, logsum, merged, hidden_pre)
    return (result, kept)


def backward_layer(grad_y, kept, params, cosine, sine):
    gain_one, bias_one, gain_two, bias_two, w_qkv, w_out, w_up, w_down = params
    feed, query_heads, key_heads, value_heads, attended, logsum, merged, hidden_pre = kept
    seqs, toks, width = feed.shape
    flat = feed.astype(single).reshape(seqs * toks, width)
    gain_a = gain_one.astype(single)
    gain_c = gain_two.astype(single)
    normed_a, unit_a, scale_a = normalize(flat, gain_a, bias_one.astype(single))
    normed_c, unit_c, scale_c = normalize(flat, gain_c, bias_two.astype(single))
    normed_a = normed_a.astype(bfloat)
    normed_c = normed_c.astype(bfloat)
    grad_flat = grad_y.reshape(seqs * toks, width)
    grad_low = grad_flat.astype(bfloat)
    grad_w_out = jnp.einsum("nd,ne->de", merged, grad_low, preferred_element_type=single)
    grad_merged = jnp.einsum("ne,de->nd", grad_low, w_out, preferred_element_type=single).astype(
        bfloat
    )
    grad_att = lax.all_to_all(
        grad_merged.reshape(seqs, toks, width), "seq", split_axis=2, concat_axis=1, tiled=True
    )
    grad_att = grad_att.reshape(query_heads.shape)
    hidden = jax.nn.gelu(hidden_pre, approximate=False).astype(bfloat)
    grad_w_down = jnp.einsum("nf,nd->fd", hidden, grad_low, preferred_element_type=single)
    grad_hidden = jnp.einsum("nd,fd->nf", grad_low, w_down, preferred_element_type=single)
    grad_pre = (grad_hidden * gelu_slope(hidden_pre)).astype(bfloat)
    grad_w_up = jnp.einsum("nd,nf->df", normed_c, grad_pre, preferred_element_type=single)
    grad_c = jnp.einsum("nf,df->nd", grad_pre, w_up, preferred_element_type=single)
    block = min(512, query_heads.shape[1])
    grad_query, grad_key, grad_value = attend_back(
        query_heads, key_heads, value_heads, grad_att, logsum, block
    )
    length = query_heads.shape[1]
    flat_heads = (seqs, length, query_heads.shape[2] * HD)
    grad_query, grad_key, grad_value = (
        lax.all_to_all(
            grad_query.astype(bfloat).reshape(flat_heads),
            "seq",
            split_axis=1,
            concat_axis=2,
            tiled=True,
        ),
        lax.all_to_all(
            grad_key.astype(bfloat).reshape(flat_heads),
            "seq",
            split_axis=1,
            concat_axis=2,
            tiled=True,
        ),
        lax.all_to_all(
            grad_value.astype(bfloat).reshape(flat_heads),
            "seq",
            split_axis=1,
            concat_axis=2,
            tiled=True,
        ),
    )
    shape_tok = (seqs, toks, H, HD)
    grad_query = rotate(grad_query.astype(single).reshape(shape_tok), cosine, sine, -1.0).reshape(
        seqs * toks, width
    )
    grad_key = rotate(grad_key.astype(single).reshape(shape_tok), cosine, sine, -1.0).reshape(
        seqs * toks, width
    )
    grad_mixed = jnp.concatenate(
        [grad_query, grad_key, grad_value.astype(single).reshape(seqs * toks, width)], axis=-1
    ).astype(bfloat)
    grad_w_qkv = jnp.einsum("nd,ne->de", normed_a, grad_mixed, preferred_element_type=single)
    grad_a = jnp.einsum("ne,de->nd", grad_mixed, w_qkv, preferred_element_type=single)
    grad_x_one, grad_gain_one, grad_bias_one = norm_back(grad_a, unit_a, scale_a, gain_a)
    grad_x_two, grad_gain_two, grad_bias_two = norm_back(grad_c, unit_c, scale_c, gain_c)
    grad_x = (grad_flat + grad_x_one + grad_x_two).reshape(seqs, toks, width)
    grads = (
        grad_gain_one,
        grad_bias_one,
        grad_gain_two,
        grad_bias_two,
        grad_w_qkv,
        grad_w_out,
        grad_w_up,
        grad_w_down,
    )
    return (grad_x, grads)


def owners_each(grads):
    shares = jax.tree.map(
        lambda part: part.astype(jnp.float32),
        lax.psum_scatter(as_sent(grads), "fsdp", scatter_dimension=0, tiled=True),
    )
    return jax.tree.map(lambda part: part.astype(jnp.float32), lax.psum(as_sent(shares), "seq"))


def on_device(
    inputs, cotangent, ln1_gain, ln1_bias, ln2_gain, ln2_bias, w_qkv, w_out, w_up, w_down
):
    section = lax.axis_index("section")
    first = section == 0
    gathered = (
        lax.all_gather(ln1_gain, "fsdp", axis=1, tiled=True),
        lax.all_gather(ln1_bias, "fsdp", axis=1, tiled=True),
        lax.all_gather(ln2_gain, "fsdp", axis=1, tiled=True),
        lax.all_gather(ln2_bias, "fsdp", axis=1, tiled=True),
        lax.all_gather(w_qkv, "fsdp", axis=1, tiled=True),
        lax.all_gather(w_out, "fsdp", axis=1, tiled=True),
        lax.all_gather(w_up, "fsdp", axis=1, tiled=True),
        lax.all_gather(w_down, "fsdp", axis=1, tiled=True),
    )
    params = tuple((piece[0] for piece in gathered))
    micro, seqs, toks, width = inputs.shape
    positions = (lax.axis_index("seq") * toks + jnp.arange(toks)).astype(single)
    cosine, sine = rotary_tables(positions)
    incoming = jnp.zeros((seqs, toks, width), bfloat)
    result_ticks = []
    kept_ticks = []
    for tick in range(micro + 1):
        feed = jnp.where(first, inputs[min(tick, micro - 1)], incoming)
        result, kept = forward_layer(feed, params, cosine, sine)
        result_low = result.astype(bfloat)
        result_ticks.append(result_low)
        kept_ticks.append(kept)
        if tick < micro:
            incoming = from_behind(result_low, "section", 1)
    kept_all = jax.tree.map(lambda *parts: jnp.stack(parts), *kept_ticks)
    outputs = jnp.stack(
        [jnp.where(first, result_ticks[index], result_ticks[index + 1]) for index in range(micro)]
    )
    owned = tuple(
        (
            jnp.zeros((piece.shape[0] // lax.axis_size("fsdp"),) + piece.shape[1:], single)
            for piece in params
        )
    )
    back_in = jnp.zeros((seqs, toks, width), bfloat)
    grad_ticks = []
    for tick in range(micro + 1):
        slot = jnp.clip(tick - 1 + 2 * section, 0, micro)
        kept = jax.tree.map(
            lambda arr: lax.dynamic_index_in_dim(arr, slot, 0, keepdims=False), kept_all
        )
        grad_y = jnp.where(first, back_in, cotangent[min(tick, micro - 1)]).astype(single)
        grad_x, grads = backward_layer(grad_y, kept, params, cosine, sine)
        member = tick - 1 + section
        valid = ((member >= 0) & (member < micro)).astype(single)
        grads = tuple((piece * valid for piece in grads))
        owned = tuple((left + right for left, right in zip(owned, owners_each(grads))))
        grad_low = grad_x.astype(bfloat)
        grad_ticks.append(grad_low)
        if tick < micro:
            back_in = from_behind(grad_low, "section", -1)
    input_grads = jnp.stack(
        [jnp.where(first, grad_ticks[index + 1], grad_ticks[index]) for index in range(micro)]
    )
    shaped = tuple((piece[None] for piece in owned))
    return (outputs[None], input_grads[None]) + shaped


NEG = float("-inf")


def dot(left, right, dims=((1,), (0,))):
    return lax.dot_general(left, right, (dims, ((), ())), preferred_element_type=single)


def head_tables(length, lanes):
    cosine, sine = rotary_tables(jnp.arange(length).astype(single))
    half = ROT // 2
    rest = HD - ROT
    ones = jnp.ones((length, rest), single)
    zeros = jnp.zeros((length, rest), single)
    none = jnp.zeros((length, half), single)
    keep = jnp.concatenate([cosine, cosine, ones], axis=-1)
    upper = jnp.concatenate([-sine, none, zeros], axis=-1)
    lower = jnp.concatenate([none, sine, zeros], axis=-1)
    return tuple(jnp.tile(part, (1, lanes // HD)) for part in (keep, upper, lower))


def turn(block, keep, upper, lower):
    half = ROT // 2
    lanes = block.shape[-1]
    return (
        block * keep
        + pltpu.roll(block, lanes - half, 1) * upper
        + pltpu.roll(block, half, 1) * lower
    )


def turn_back(block, keep, upper, lower):
    return turn(block, keep, -upper, -lower)


def attend_kernel(rows, q_ref, k_ref, v_ref, keep_ref, up_ref, low_ref, o_ref):
    length, lanes = q_ref.shape
    keep, upper, lower = keep_ref[...], up_ref[...], low_ref[...]
    query = (turn(q_ref[...], keep, upper, lower).astype(bfloat).astype(single) * HD**-0.5).astype(
        bfloat
    )
    key = turn(k_ref[...], keep, upper, lower).astype(bfloat)
    value = v_ref[...].astype(bfloat)
    lane = lax.broadcasted_iota(jnp.int32, (rows, lanes), 1) // HD
    below = lax.broadcasted_iota(jnp.int32, (rows, rows), 1) <= lax.broadcasted_iota(
        jnp.int32, (rows, rows), 0
    )
    nt = ((1,), (1,))
    for start in range(0, length, rows):
        out = jnp.zeros((rows, lanes), single)
        for head in range(lanes // HD):
            mine = lane == head
            part = jnp.where(mine, query[start : start + rows], jnp.zeros((), bfloat))
            diag = jnp.where(below, dot(part, key[start : start + rows], nt), NEG)
            top = jnp.max(diag, axis=-1, keepdims=True)
            if start:
                full = dot(part, key[:start], nt)
                top = jnp.maximum(top, jnp.max(full, axis=-1, keepdims=True))
                full = jnp.exp(full - top)
            diag = jnp.exp(diag - top)
            total = jnp.sum(diag, axis=-1, keepdims=True)
            got = dot(diag.astype(bfloat), value[start : start + rows])
            if start:
                total = total + jnp.sum(full, axis=-1, keepdims=True)
                got = got + dot(full.astype(bfloat), value[:start])
            out = jnp.where(mine, got * (1.0 / total), out)
        o_ref[start : start + rows, :] = out.astype(bfloat)


def attend_back_kernel(
    rows, q_ref, k_ref, v_ref, go_ref, keep_ref, up_ref, low_ref, out_ref, gk_ref, gv_ref
):
    pair = pl.program_id(0)
    length, lanes = q_ref.shape
    width = out_ref.shape[1] // 3
    scale = HD**-0.5
    keep, upper, lower = keep_ref[...], up_ref[...], low_ref[...]
    query = (turn(q_ref[...], keep, upper, lower).astype(bfloat).astype(single) * scale).astype(
        bfloat
    )
    key = turn(k_ref[...], keep, upper, lower).astype(bfloat)
    value = v_ref[...].astype(bfloat)
    gk_ref[...] = jnp.zeros_like(gk_ref)
    gv_ref[...] = jnp.zeros_like(gv_ref)
    lane = lax.broadcasted_iota(jnp.int32, (rows, lanes), 1) // HD
    above = lax.broadcasted_iota(jnp.int32, (rows, rows), 0) <= lax.broadcasted_iota(
        jnp.int32, (rows, rows), 1
    )
    nt = ((1,), (1,))
    tn = ((0,), (0,))
    zero = jnp.zeros((), bfloat)
    for start in range(0, length, rows):
        here = slice(start, start + rows)
        out = jnp.zeros((rows, lanes), single)
        for head in range(lanes // HD):
            mine = lane == head
            part = jnp.where(mine, query[here], zero)
            grad = jnp.where(mine, go_ref[here, :], zero)
            diag = jnp.where(above, dot(key[here], part, nt), NEG)
            top = jnp.max(diag, axis=0, keepdims=True)
            if start:
                full = dot(key[:start], part, nt)
                top = jnp.maximum(top, jnp.max(full, axis=0, keepdims=True))
                full = jnp.exp(full - top)
            diag = jnp.exp(diag - top)
            total = jnp.sum(diag, axis=0, keepdims=True)
            if start:
                total = total + jnp.sum(full, axis=0, keepdims=True)
            share = 1.0 / total
            diag = diag * share
            grad_diag = dot(value[here], grad, nt)
            delta = jnp.sum(diag * grad_diag, axis=0, keepdims=True)
            if start:
                full = full * share
                grad_full = dot(value[:start], grad, nt)
                delta = delta + jnp.sum(full * grad_full, axis=0, keepdims=True)
            score_diag = (diag * (grad_diag - delta)).astype(bfloat)
            got = dot(score_diag, key[here], tn)
            gv_ref[here, :] += dot(diag.astype(bfloat), grad)
            gk_ref[here, :] += dot(score_diag, part)
            if start:
                score_full = (full * (grad_full - delta)).astype(bfloat)
                got = got + dot(score_full, key[:start], tn)
                gv_ref[:start, :] += dot(full.astype(bfloat), grad)
                gk_ref[:start, :] += dot(score_full, part)
            out = jnp.where(mine, got * scale, out)
        out = turn_back(out.astype(bfloat).astype(single), keep[here], upper[here], lower[here])
        out_ref[here, pl.ds(pl.multiple_of(pair * lanes, lanes), lanes)] = out.astype(bfloat)
    back = turn_back(gk_ref[...].astype(bfloat).astype(single), keep, upper, lower)
    out_ref[:, pl.ds(pl.multiple_of(width + pair * lanes, lanes), lanes)] = back.astype(bfloat)
    out_ref[:, pl.ds(pl.multiple_of(2 * width + pair * lanes, lanes), lanes)] = gv_ref[
        ...
    ].astype(bfloat)


TILE = 2 * HD


def attend_whole(mixed, tables):
    length, wide = mixed.shape
    width = wide // 3
    pairs = width // TILE
    rows = min(256, length)
    table = pl.BlockSpec((length, TILE), lambda p: (0, 0))
    return pl.pallas_call(
        functools.partial(attend_kernel, rows),
        grid=(pairs,),
        in_specs=[
            pl.BlockSpec((length, TILE), lambda p: (0, p)),
            pl.BlockSpec((length, TILE), lambda p: (0, pairs + p)),
            pl.BlockSpec((length, TILE), lambda p: (0, 2 * pairs + p)),
            table,
            table,
            table,
        ],
        out_specs=pl.BlockSpec((length, TILE), lambda p: (0, p)),
        out_shape=jax.ShapeDtypeStruct((length, width), bfloat),
        cost_estimate=pl.CostEstimate(
            flops=4 * length * length * width,
            bytes_accessed=14 * length * width,
            transcendentals=length * length * width // HD,
        ),
        name="attend",
    )(mixed, mixed, mixed, *tables)


def attend_back_whole(mixed, grad_out, tables):
    length, wide = mixed.shape
    width = wide // 3
    pairs = width // TILE
    rows = min(256, length)
    table = pl.BlockSpec((length, TILE), lambda p: (0, 0))
    return pl.pallas_call(
        functools.partial(attend_back_kernel, rows),
        grid=(pairs,),
        in_specs=[
            pl.BlockSpec((length, TILE), lambda p: (0, p)),
            pl.BlockSpec((length, TILE), lambda p: (0, pairs + p)),
            pl.BlockSpec((length, TILE), lambda p: (0, 2 * pairs + p)),
            pl.BlockSpec((length, TILE), lambda p: (0, p)),
            table,
            table,
            table,
        ],
        out_specs=pl.BlockSpec((length, wide), lambda p: (0, 0)),
        out_shape=jax.ShapeDtypeStruct((length, wide), bfloat),
        scratch_shapes=[
            pltpu.VMEM((length, TILE), single),
            pltpu.VMEM((length, TILE), single),
        ],
        cost_estimate=pl.CostEstimate(
            flops=10 * length * length * width,
            bytes_accessed=20 * length * width,
            transcendentals=length * length * width // HD,
        ),
        name="attend_back",
    )(mixed, mixed, mixed, grad_out, *tables)


SWAP = [(0, 1), (1, 0)]
XPAIR = [(0, 1), (1, 0), (2, 3), (3, 2)]
YPAIR = [(0, 2), (2, 0), (1, 3), (3, 1)]


def over_x(value):
    return lax.ppermute(value, "fsdp", XPAIR)


def over_y(value):
    return lax.ppermute(value, "fsdp", YPAIR)


def over_core(value):
    return lax.ppermute(value, "section", SWAP)


def collect(piece, place):
    half = piece.shape[0] // 2
    from_x = over_x(piece)
    from_y = over_y(piece)
    corner_low = over_y(from_x[:half])
    corner_high = over_x(from_y[half:])
    whole = jnp.zeros((4,) + piece.shape, piece.dtype)
    tail = (0,) * (piece.ndim - 1)
    for part, owner, row in (
        (piece, place, 0),
        (from_x, place ^ 1, 0),
        (from_y, place ^ 2, 0),
        (corner_low, place ^ 3, 0),
        (corner_high, place ^ 3, half),
    ):
        whole = lax.dynamic_update_slice(whole, part[None], (owner, row) + tail)
    return whole


def owner_block(blocks, owner, low, high):
    size = (1, high - low) + blocks.shape[2:]
    start = (owner, low) + (0,) * (blocks.ndim - 2)
    return lax.dynamic_slice(blocks, start, size)[0]


def add_low(left, right):
    return (left.astype(single) + right.astype(single)).astype(bfloat)


def reduce_owned(blocks, place, line):
    rows = blocks.shape[1]
    half = rows // 2
    block = functools.partial(owner_block, blocks)
    got_a = over_x(jnp.stack([block(place ^ 1, 0, half), block(place ^ 3, 0, half)]))
    got_b = over_y(jnp.stack([block(place ^ 2, half, rows), block(place ^ 3, half, rows)]))
    pass_a = over_y(add_low(block(place ^ 2, 0, half), got_a[1]))
    pass_b = over_x(add_low(block(place ^ 1, half, rows), got_b[1]))
    sum_a = block(place, 0, half).astype(single) + got_a[0].astype(single) + pass_a.astype(single)
    sum_b = block(place, half, rows).astype(single) + got_b[0].astype(single) + pass_b.astype(single)
    mine = jnp.concatenate([sum_a, sum_b]).astype(bfloat)
    inward = lax.ppermute(mine, "seq", [(0, 1), (3, 2)])
    side = add_low(mine, inward)
    across = lax.ppermute(side, "seq", [(1, 2), (2, 1)])
    total = add_low(side, across)
    outward = lax.ppermute(total, "seq", [(1, 0), (2, 3)])
    return jnp.where((line == 0) | (line == 3), outward, total)


def layer_forward(x_low, params, tables):
    gain_one, bias_one, gain_two, bias_two, w_qkv, w_out, w_up, w_down = params
    flat = x_low.astype(single)
    mean = jnp.mean(flat, axis=-1, keepdims=True)
    cent = flat - mean
    scale = lax.rsqrt(jnp.mean(cent * cent, axis=-1, keepdims=True) + eps_norm)
    unit = cent * scale
    normed_a = (unit * gain_one + bias_one).astype(bfloat)
    normed_c = (unit * gain_two + bias_two).astype(bfloat)
    mixed = dot(normed_a, w_qkv)
    attended = attend_whole(mixed, tables)
    pre = dot(normed_c, w_up)
    phi = 0.5 * (1.0 + lax.erf(pre * (1.0 / math.sqrt(2.0))))
    hidden = (pre * phi).astype(bfloat)
    slope = (phi + pre * jnp.exp(-0.5 * pre * pre) * (1.0 / math.sqrt(2.0 * math.pi))).astype(
        bfloat
    )
    partial = (dot(attended, w_out) + dot(hidden, w_down)).astype(bfloat)
    other = over_core(partial)
    result = (flat + (partial.astype(single) + other.astype(single))).astype(bfloat)
    kept = (x_low, mean, scale, normed_a, normed_c, mixed, attended, hidden, slope)
    return result, kept


def layer_backward(grad_low, kept, params, tables, place, line):
    gain_one, bias_one, gain_two, bias_two, w_qkv, w_out, w_up, w_down = params
    x_low, mean, scale, normed_a, normed_c, mixed, attended, hidden, slope = kept
    nt = ((1,), (1,))
    tn = ((0,), (0,))

    def owners(value):
        return value.astype(bfloat).reshape((4, value.shape[0] // 4, value.shape[1]))

    grad_w_down = owners(dot(hidden, grad_low, tn))
    grad_pre = (dot(grad_low, w_down, nt) * slope.astype(single)).astype(bfloat)
    grad_w_up = owners(dot(normed_c, grad_pre, tn))
    down = reduce_owned(grad_w_down, place, line)
    up = reduce_owned(grad_w_up, place, line)
    grad_att = dot(grad_low, w_out, nt).astype(bfloat)
    grad_mixed = attend_back_whole(mixed, grad_att, tables)
    grad_w_out = owners(dot(attended, grad_low, tn))
    grad_w_qkv = owners(dot(normed_a, grad_mixed, tn))
    wide = grad_w_out.shape[2] // 2
    out_block = jnp.concatenate([grad_w_out[:, :, :wide], grad_w_out[:, :, wide:]], axis=1)
    attn = reduce_owned(jnp.concatenate([grad_w_qkv, out_block], axis=2), place, line)
    grad_c = dot(grad_pre, w_up, nt)
    grad_a = dot(grad_mixed, w_qkv, nt)
    unit = (x_low.astype(single) - mean) * scale
    small = jnp.stack(
        [
            jnp.sum(grad_a * unit, axis=0),
            jnp.sum(grad_a, axis=0),
            jnp.sum(grad_c * unit, axis=0),
            jnp.sum(grad_c, axis=0),
        ]
    )
    partial = (grad_a * gain_one + grad_c * gain_two).astype(bfloat)
    other = over_core(partial)
    both = partial.astype(single) + other.astype(single)
    inner = (
        both
        - jnp.mean(both, axis=-1, keepdims=True)
        - unit * jnp.mean(both * unit, axis=-1, keepdims=True)
    )
    grad_x = (grad_low.astype(single) + scale * inner).astype(bfloat)
    return grad_x, small, (attn, up, down)


def to_sequence(blocks, core):
    count, toks, width = blocks.shape
    half = toks // 2
    mine = lax.dynamic_slice_in_dim(blocks, core * half, half, 1)
    mine = lax.all_to_all(mine, "seq", split_axis=0, concat_axis=0, tiled=True)
    other = over_core(mine)
    first = jnp.where(core == 0, mine, other)
    second = jnp.where(core == 0, other, mine)
    return jnp.stack([first, second], axis=1).reshape(count * toks, width)


def from_sequence(whole, count, core, owner):
    length, width = whole.shape
    half = length // count // 2
    blocks = whole.reshape(count, 2, half, width)
    mine = lax.dynamic_index_in_dim(blocks, core, 1, keepdims=False)
    mine = lax.all_to_all(mine, "seq", split_axis=0, concat_axis=0, tiled=True)
    other = lax.ppermute(mine, "section", [(1 - owner, owner)])
    pair = (mine, other) if owner == 0 else (other, mine)
    return jnp.stack(pair, axis=1).reshape(count, 2 * half, width)


def halves(core, w_qkv, w_out, w_up, w_down):
    take = functools.partial(lax.dynamic_index_in_dim, index=core, keepdims=False)
    rows, wide = w_qkv.shape
    qkv = take(w_qkv.reshape(rows, 3, 4, 2, wide // 24), axis=3).reshape(rows, wide // 2)
    out = take(w_out.reshape(2, w_out.shape[0] // 2, w_out.shape[1]), axis=0)
    up = take(w_up.reshape(rows, 4, 2, w_up.shape[1] // 8), axis=2).reshape(
        rows, w_up.shape[1] // 2
    )
    down = take(w_down.reshape(2, w_down.shape[0] // 2, w_down.shape[1]), axis=0)
    wide = out.shape[1] // 2
    attn = jnp.concatenate([qkv, jnp.concatenate([out[:, :wide], out[:, wide:]], axis=0)], axis=1)
    return attn, up, down


def on_chip(inputs, cotangent, ln1_gain, ln1_bias, ln2_gain, ln2_bias, w_qkv, w_out, w_up, w_down):
    core = lax.axis_index("section")
    line = lax.axis_index("seq")
    place = lax.axis_index("fsdp")
    micro, seqs, toks, width = inputs.shape
    count = micro * seqs
    x_low = to_sequence(inputs.reshape(count, toks, width), core)
    small = jnp.stack([ln1_gain[0], ln1_bias[0], ln2_gain[0], ln2_bias[0]])
    small = lax.all_gather(small, ("section", "fsdp")).reshape(2, 4, 4, small.shape[1])
    small = small.transpose(0, 2, 1, 3).reshape(2, 4, width).astype(single)
    shards = (w_qkv[0], w_out[0], w_up[0], w_down[0])
    mine = halves(core, *shards)
    other = tuple(over_core(piece) for piece in halves(1 - core, *shards))
    tables = head_tables(x_low.shape[0], TILE)
    qkv_wide = w_qkv.shape[2] // 2
    layers = []
    for layer in range(2):
        pieces = tuple(
            jnp.where(core == layer, own, given) for own, given in zip(mine, other)
        )
        attn, up, down = (collect(piece, place) for piece in pieces)
        qkv = attn[:, :, :qkv_wide].reshape(width, qkv_wide)
        rows = attn.shape[1] // 2
        out = jnp.concatenate([attn[:, :rows, qkv_wide:], attn[:, rows:, qkv_wide:]], axis=2)
        layers.append(
            tuple(small[layer])
            + (
                qkv,
                out.reshape(4 * rows, width),
                up.reshape(width, up.shape[2]),
                down.reshape(4 * down.shape[1], width),
            )
        )
    mid, kept_one = layer_forward(x_low, layers[0], tables)
    last, kept_two = layer_forward(mid, layers[1], tables)
    grad_last = to_sequence(cotangent.reshape(count, toks, width), core)
    shape = (micro, seqs, toks, width)
    out_one = from_sequence(mid, count, core, 0).reshape(shape)
    out_two = from_sequence(last, count, core, 1).reshape(shape)
    grad_mid, small_two, owned_two = layer_backward(
        grad_last, kept_two, layers[1], tables, place, line
    )
    grad_two = from_sequence(grad_mid, count, core, 1).reshape(shape)
    grad_first, small_one, owned_one = layer_backward(
        grad_mid, kept_one, layers[0], tables, place, line
    )
    grad_one = from_sequence(grad_first, count, core, 0).reshape(shape)
    first = core == 0
    outputs = jnp.where(first, out_one, out_two)[None]
    input_grads = jnp.where(first, grad_one, grad_two)[None]
    sums = lax.psum(jnp.stack([small_one, small_two]), ("section", "seq", "fsdp"))
    sums = lax.dynamic_index_in_dim(sums, core, 0, keepdims=False)
    block = width // 4
    sums = lax.dynamic_slice_in_dim(sums, place * block, block, 1)
    low_half, high_half = [], []
    for one, two in zip(owned_one, owned_two):
        given = lax.ppermute(one, "section", [(1, 0)])
        taken = lax.ppermute(two, "section", [(0, 1)])
        low_half.append(jnp.where(first, one, taken).astype(single))
        high_half.append(jnp.where(first, given, two).astype(single))
    (attn_low, up_low, down_low), (attn_high, up_high, down_high) = low_half, high_half
    rows = attn_low.shape[0]

    def columns(low, high, groups):
        size = low.shape[1] // groups
        pair = jnp.stack(
            [low.reshape(rows, groups, size), high.reshape(rows, groups, size)], axis=2
        )
        return pair.reshape(1, rows, -1)

    def out_rows(value):
        part = value[:, qkv_wide:]
        return jnp.concatenate([part[: rows // 2], part[rows // 2 :]], axis=1)

    grad_qkv = columns(attn_low[:, :qkv_wide], attn_high[:, :qkv_wide], 12)
    grad_out = jnp.concatenate([out_rows(attn_low), out_rows(attn_high)])[None]
    grad_up = columns(up_low, up_high, 4)
    grad_down = jnp.concatenate([down_low, down_high])[None]
    norms = tuple(sums[index][None] for index in range(4))
    return (outputs, input_grads) + norms + (grad_qkv, grad_out, grad_up, grad_down)


def on_any(inputs, *rest):
    micro, seqs, toks, _ = inputs.shape
    sizes = (lax.axis_size("section"), lax.axis_size("seq"), lax.axis_size("fsdp"))
    if sizes == (2, 4, 4) and micro * seqs == 4 and toks % 64 == 0:
        return on_chip(inputs, *rest)
    return on_device(inputs, *rest)


def solution(mesh):
    in_specs = (
        P(None, "fsdp", "seq", None),
        P(None, "fsdp", "seq", None),
        P("section", "fsdp"),
        P("section", "fsdp"),
        P("section", "fsdp"),
        P("section", "fsdp"),
        P("section", "fsdp", None),
        P("section", "fsdp", None),
        P("section", "fsdp", None),
        P("section", "fsdp", None),
    )
    out_specs = (
        P("section", None, "fsdp", "seq", None),
        P("section", None, "fsdp", "seq", None),
        P("section", "fsdp"),
        P("section", "fsdp"),
        P("section", "fsdp"),
        P("section", "fsdp"),
        P("section", "fsdp", None),
        P("section", "fsdp", None),
        P("section", "fsdp", None),
        P("section", "fsdp", None),
    )
    return jax.shard_map(
        on_any, mesh=mesh, in_specs=in_specs, out_specs=out_specs, check_vma=False
    )
```

```python
import functools
import math

import jax
import jax.numpy as jnp
from jax import lax
from jax.experimental import pallas as pl
from jax.experimental.pallas import tpu as pltpu
from jax.sharding import PartitionSpec as P

H = 16
HD = 64
ROT = 16


eps_norm = 1e-05
rope_base = 10000.0
bfloat = jnp.bfloat16
single = jnp.float32


def as_sent(value):
    return jax.tree.map(lambda a: a.astype(jnp.bfloat16) if a.dtype == jnp.float32 else a, value)


def from_behind(block, axis, distance):
    devices = range(lax.axis_size(axis))
    route = [(i - distance, i) for i in devices if i - distance in devices]
    return lax.ppermute(block, axis, route)


def normalize(xval, gain, shift):
    mean = jnp.mean(xval, axis=-1, keepdims=True)
    cent = xval - mean
    scale = lax.rsqrt(jnp.mean(cent * cent, axis=-1, keepdims=True) + eps_norm)
    unit = cent * scale
    return (unit * gain + shift, unit, scale)


def norm_back(grad, unit, scale, gain):
    dunit = grad * gain
    inner = (
        dunit
        - jnp.mean(dunit, axis=-1, keepdims=True)
        - unit * jnp.mean(dunit * unit, axis=-1, keepdims=True)
    )
    return (scale * inner, jnp.sum(grad * unit, axis=0), jnp.sum(grad, axis=0))


def rotary_tables(positions):
    freqs = jnp.power(rope_base, -jnp.arange(0, ROT, 2).astype(single) / ROT)
    angles = positions[:, None] * freqs[None, :]
    return (jnp.cos(angles), jnp.sin(angles))


def rotate(block, cosine, sine, sign):
    half = ROT // 2
    first = block[..., :half]
    second = block[..., half:ROT]
    cos_b = cosine[:, None, :]
    sin_b = sine[:, None, :] * sign
    return jnp.concatenate(
        [first * cos_b - second * sin_b, second * cos_b + first * sin_b, block[..., ROT:]], axis=-1
    )


def gelu_slope(value):
    return 0.5 * (1.0 + lax.erf(value * (1.0 / math.sqrt(2.0)))) + value * jnp.exp(
        -0.5 * value * value
    ) * (1.0 / math.sqrt(2.0 * math.pi))


def block_scores(query_blk, key_heads, start):
    block = query_blk.shape[1]
    length = key_heads.shape[1]
    scores = jnp.einsum("sqhd,skhd->shqk", query_blk, key_heads, preferred_element_type=single) * (
        1.0 / math.sqrt(HD)
    )
    query_pos = start + jnp.arange(block)
    key_pos = jnp.arange(length)
    return jnp.where(key_pos[None, :] <= query_pos[:, None], scores, -jnp.inf)


def attend(query_heads, key_heads, value_heads, block):
    seqs, length, local, size = query_heads.shape
    count = length // block

    def one_block(start):
        query_blk = lax.dynamic_slice_in_dim(query_heads, start, block, 1)
        scores = block_scores(query_blk, key_heads, start)
        top = jnp.max(scores, axis=-1, keepdims=True)
        expd = jnp.exp(scores - top)
        total = jnp.sum(expd, axis=-1, keepdims=True)
        probs = (expd / total).astype(bfloat)
        out = jnp.einsum("shqk,skhd->sqhd", probs, value_heads, preferred_element_type=single)
        return (out.astype(bfloat), top[..., 0] + jnp.log(total[..., 0]))

    outs, logsum = lax.map(one_block, jnp.arange(count) * block)
    outs = outs.transpose(1, 0, 2, 3, 4).reshape(seqs, length, local, size)
    return (outs, logsum)


def attend_back(query_heads, key_heads, value_heads, grad_out, logsum, block):
    seqs, length, local, size = query_heads.shape
    count = length // block
    scale = 1.0 / math.sqrt(size)

    def step(carry, item):
        grad_key, grad_value = carry
        start, logsum_blk = item
        query_blk = lax.dynamic_slice_in_dim(query_heads, start, block, 1)
        grad_blk = lax.dynamic_slice_in_dim(grad_out, start, block, 1)
        scores = block_scores(query_blk, key_heads, start)
        probs = jnp.exp(scores - logsum_blk[..., None])
        grad_probs = jnp.einsum(
            "sqhd,skhd->shqk", grad_blk, value_heads, preferred_element_type=single
        )
        delta = jnp.sum(probs * grad_probs, axis=-1, keepdims=True)
        grad_scores = (probs * (grad_probs - delta)).astype(bfloat)
        grad_query = (
            jnp.einsum("shqk,skhd->sqhd", grad_scores, key_heads, preferred_element_type=single)
            * scale
        )
        grad_key = (
            grad_key
            + jnp.einsum("shqk,sqhd->skhd", grad_scores, query_blk, preferred_element_type=single)
            * scale
        )
        grad_value = grad_value + jnp.einsum(
            "shqk,sqhd->skhd", probs.astype(bfloat), grad_blk, preferred_element_type=single
        )
        return ((grad_key, grad_value), grad_query)

    zeros = jnp.zeros((seqs, length, local, size), single)
    (grad_key, grad_value), grad_query = lax.scan(
        step, (zeros, zeros), (jnp.arange(count) * block, logsum)
    )
    grad_query = grad_query.transpose(1, 0, 2, 3, 4).reshape(seqs, length, local, size)
    return (grad_query, grad_key, grad_value)


def forward_layer(feed, params, cosine, sine):
    gain_one, bias_one, gain_two, bias_two, w_qkv, w_out, w_up, w_down = params
    seqs, toks, width = feed.shape
    flat = feed.astype(single).reshape(seqs * toks, width)
    normed_a, _, _ = normalize(flat, gain_one.astype(single), bias_one.astype(single))
    normed_c, _, _ = normalize(flat, gain_two.astype(single), bias_two.astype(single))
    mixed = jnp.dot(normed_a.astype(bfloat), w_qkv, preferred_element_type=single).reshape(
        seqs, toks, 3, H, HD
    )
    query = rotate(mixed[:, :, 0], cosine, sine, 1.0).astype(bfloat).reshape(seqs, toks, width)
    key = rotate(mixed[:, :, 1], cosine, sine, 1.0).astype(bfloat).reshape(seqs, toks, width)
    value = mixed[:, :, 2].astype(bfloat).reshape(seqs, toks, width)
    query_heads, key_heads, value_heads = (
        lax.all_to_all(query, "seq", split_axis=2, concat_axis=1, tiled=True),
        lax.all_to_all(key, "seq", split_axis=2, concat_axis=1, tiled=True),
        lax.all_to_all(value, "seq", split_axis=2, concat_axis=1, tiled=True),
    )
    length = query_heads.shape[1]
    local = query_heads.shape[2] // HD
    shape_heads = (seqs, length, local, HD)
    query_heads = query_heads.reshape(shape_heads)
    key_heads = key_heads.reshape(shape_heads)
    value_heads = value_heads.reshape(shape_heads)
    block = min(512, length)
    attended, logsum = attend(query_heads, key_heads, value_heads, block)
    merged = lax.all_to_all(
        attended.reshape(seqs, length, local * HD), "seq", split_axis=1, concat_axis=2, tiled=True
    )
    merged = merged.reshape(seqs * toks, width)
    attn = jnp.dot(merged, w_out, preferred_element_type=single)
    hidden_pre = jnp.dot(normed_c.astype(bfloat), w_up, preferred_element_type=single)
    hidden = jax.nn.gelu(hidden_pre, approximate=False).astype(bfloat)
    mlp = jnp.dot(hidden, w_down, preferred_element_type=single)
    result = (flat + attn + mlp).reshape(seqs, toks, width)
    kept = (feed, query_heads, key_heads, value_heads, attended, logsum, merged, hidden_pre)
    return (result, kept)


def backward_layer(grad_y, kept, params, cosine, sine):
    gain_one, bias_one, gain_two, bias_two, w_qkv, w_out, w_up, w_down = params
    feed, query_heads, key_heads, value_heads, attended, logsum, merged, hidden_pre = kept
    seqs, toks, width = feed.shape
    flat = feed.astype(single).reshape(seqs * toks, width)
    gain_a = gain_one.astype(single)
    gain_c = gain_two.astype(single)
    normed_a, unit_a, scale_a = normalize(flat, gain_a, bias_one.astype(single))
    normed_c, unit_c, scale_c = normalize(flat, gain_c, bias_two.astype(single))
    normed_a = normed_a.astype(bfloat)
    normed_c = normed_c.astype(bfloat)
    grad_flat = grad_y.reshape(seqs * toks, width)
    grad_low = grad_flat.astype(bfloat)
    grad_w_out = jnp.einsum("nd,ne->de", merged, grad_low, preferred_element_type=single)
    grad_merged = jnp.einsum("ne,de->nd", grad_low, w_out, preferred_element_type=single).astype(
        bfloat
    )
    grad_att = lax.all_to_all(
        grad_merged.reshape(seqs, toks, width), "seq", split_axis=2, concat_axis=1, tiled=True
    )
    grad_att = grad_att.reshape(query_heads.shape)
    hidden = jax.nn.gelu(hidden_pre, approximate=False).astype(bfloat)
    grad_w_down = jnp.einsum("nf,nd->fd", hidden, grad_low, preferred_element_type=single)
    grad_hidden = jnp.einsum("nd,fd->nf", grad_low, w_down, preferred_element_type=single)
    grad_pre = (grad_hidden * gelu_slope(hidden_pre)).astype(bfloat)
    grad_w_up = jnp.einsum("nd,nf->df", normed_c, grad_pre, preferred_element_type=single)
    grad_c = jnp.einsum("nf,df->nd", grad_pre, w_up, preferred_element_type=single)
    block = min(512, query_heads.shape[1])
    grad_query, grad_key, grad_value = attend_back(
        query_heads, key_heads, value_heads, grad_att, logsum, block
    )
    length = query_heads.shape[1]
    flat_heads = (seqs, length, query_heads.shape[2] * HD)
    grad_query, grad_key, grad_value = (
        lax.all_to_all(
            grad_query.astype(bfloat).reshape(flat_heads),
            "seq",
            split_axis=1,
            concat_axis=2,
            tiled=True,
        ),
        lax.all_to_all(
            grad_key.astype(bfloat).reshape(flat_heads),
            "seq",
            split_axis=1,
            concat_axis=2,
            tiled=True,
        ),
        lax.all_to_all(
            grad_value.astype(bfloat).reshape(flat_heads),
            "seq",
            split_axis=1,
            concat_axis=2,
            tiled=True,
        ),
    )
    shape_tok = (seqs, toks, H, HD)
    grad_query = rotate(grad_query.astype(single).reshape(shape_tok), cosine, sine, -1.0).reshape(
        seqs * toks, width
    )
    grad_key = rotate(grad_key.astype(single).reshape(shape_tok), cosine, sine, -1.0).reshape(
        seqs * toks, width
    )
    grad_mixed = jnp.concatenate(
        [grad_query, grad_key, grad_value.astype(single).reshape(seqs * toks, width)], axis=-1
    ).astype(bfloat)
    grad_w_qkv = jnp.einsum("nd,ne->de", normed_a, grad_mixed, preferred_element_type=single)
    grad_a = jnp.einsum("ne,de->nd", grad_mixed, w_qkv, preferred_element_type=single)
    grad_x_one, grad_gain_one, grad_bias_one = norm_back(grad_a, unit_a, scale_a, gain_a)
    grad_x_two, grad_gain_two, grad_bias_two = norm_back(grad_c, unit_c, scale_c, gain_c)
    grad_x = (grad_flat + grad_x_one + grad_x_two).reshape(seqs, toks, width)
    grads = (
        grad_gain_one,
        grad_bias_one,
        grad_gain_two,
        grad_bias_two,
        grad_w_qkv,
        grad_w_out,
        grad_w_up,
        grad_w_down,
    )
    return (grad_x, grads)


def owners_each(grads):
    shares = jax.tree.map(
        lambda part: part.astype(jnp.float32),
        lax.psum_scatter(as_sent(grads), "fsdp", scatter_dimension=0, tiled=True),
    )
    return jax.tree.map(lambda part: part.astype(jnp.float32), lax.psum(as_sent(shares), "seq"))


def on_device(
    inputs, cotangent, ln1_gain, ln1_bias, ln2_gain, ln2_bias, w_qkv, w_out, w_up, w_down
):
    section = lax.axis_index("section")
    first = section == 0
    gathered = (
        lax.all_gather(ln1_gain, "fsdp", axis=1, tiled=True),
        lax.all_gather(ln1_bias, "fsdp", axis=1, tiled=True),
        lax.all_gather(ln2_gain, "fsdp", axis=1, tiled=True),
        lax.all_gather(ln2_bias, "fsdp", axis=1, tiled=True),
        lax.all_gather(w_qkv, "fsdp", axis=1, tiled=True),
        lax.all_gather(w_out, "fsdp", axis=1, tiled=True),
        lax.all_gather(w_up, "fsdp", axis=1, tiled=True),
        lax.all_gather(w_down, "fsdp", axis=1, tiled=True),
    )
    params = tuple((piece[0] for piece in gathered))
    micro, seqs, toks, width = inputs.shape
    positions = (lax.axis_index("seq") * toks + jnp.arange(toks)).astype(single)
    cosine, sine = rotary_tables(positions)
    incoming = jnp.zeros((seqs, toks, width), bfloat)
    result_ticks = []
    kept_ticks = []
    for tick in range(micro + 1):
        feed = jnp.where(first, inputs[min(tick, micro - 1)], incoming)
        result, kept = forward_layer(feed, params, cosine, sine)
        result_low = result.astype(bfloat)
        result_ticks.append(result_low)
        kept_ticks.append(kept)
        if tick < micro:
            incoming = from_behind(result_low, "section", 1)
    kept_all = jax.tree.map(lambda *parts: jnp.stack(parts), *kept_ticks)
    outputs = jnp.stack(
        [jnp.where(first, result_ticks[index], result_ticks[index + 1]) for index in range(micro)]
    )
    owned = tuple(
        (
            jnp.zeros((piece.shape[0] // lax.axis_size("fsdp"),) + piece.shape[1:], single)
            for piece in params
        )
    )
    back_in = jnp.zeros((seqs, toks, width), bfloat)
    grad_ticks = []
    for tick in range(micro + 1):
        slot = jnp.clip(tick - 1 + 2 * section, 0, micro)
        kept = jax.tree.map(
            lambda arr: lax.dynamic_index_in_dim(arr, slot, 0, keepdims=False), kept_all
        )
        grad_y = jnp.where(first, back_in, cotangent[min(tick, micro - 1)]).astype(single)
        grad_x, grads = backward_layer(grad_y, kept, params, cosine, sine)
        member = tick - 1 + section
        valid = ((member >= 0) & (member < micro)).astype(single)
        grads = tuple((piece * valid for piece in grads))
        owned = tuple((left + right for left, right in zip(owned, owners_each(grads))))
        grad_low = grad_x.astype(bfloat)
        grad_ticks.append(grad_low)
        if tick < micro:
            back_in = from_behind(grad_low, "section", -1)
    input_grads = jnp.stack(
        [jnp.where(first, grad_ticks[index + 1], grad_ticks[index]) for index in range(micro)]
    )
    shaped = tuple((piece[None] for piece in owned))
    return (outputs[None], input_grads[None]) + shaped


NEG = float("-inf")


def dot(left, right, dims=((1,), (0,))):
    return lax.dot_general(left, right, (dims, ((), ())), preferred_element_type=single)


def head_tables(length, lanes):
    cosine, sine = rotary_tables(jnp.arange(length).astype(single))
    half = ROT // 2
    rest = HD - ROT
    ones = jnp.ones((length, rest), single)
    zeros = jnp.zeros((length, rest), single)
    none = jnp.zeros((length, half), single)
    keep = jnp.concatenate([cosine, cosine, ones], axis=-1)
    upper = jnp.concatenate([-sine, none, zeros], axis=-1)
    lower = jnp.concatenate([none, sine, zeros], axis=-1)
    return tuple(jnp.tile(part, (1, lanes // HD)) for part in (keep, upper, lower))


def turn(block, keep, upper, lower):
    half = ROT // 2
    lanes = block.shape[-1]
    return (
        block * keep
        + pltpu.roll(block, lanes - half, 1) * upper
        + pltpu.roll(block, half, 1) * lower
    )


def turn_back(block, keep, upper, lower):
    return turn(block, keep, -upper, -lower)


def attend_kernel(rows, q_ref, k_ref, v_ref, keep_ref, up_ref, low_ref, o_ref):
    length, lanes = q_ref.shape
    keep, upper, lower = keep_ref[...], up_ref[...], low_ref[...]
    query = (turn(q_ref[...], keep, upper, lower).astype(bfloat).astype(single) * HD**-0.5).astype(
        bfloat
    )
    key = turn(k_ref[...], keep, upper, lower).astype(bfloat)
    value = v_ref[...].astype(bfloat)
    lane = lax.broadcasted_iota(jnp.int32, (rows, lanes), 1) // HD
    below = lax.broadcasted_iota(jnp.int32, (rows, rows), 1) <= lax.broadcasted_iota(
        jnp.int32, (rows, rows), 0
    )
    nt = ((1,), (1,))
    for start in range(0, length, rows):
        out = jnp.zeros((rows, lanes), single)
        for head in range(lanes // HD):
            mine = lane == head
            part = jnp.where(mine, query[start : start + rows], jnp.zeros((), bfloat))
            diag = jnp.where(below, dot(part, key[start : start + rows], nt), NEG)
            top = jnp.max(diag, axis=-1, keepdims=True)
            if start:
                full = dot(part, key[:start], nt)
                top = jnp.maximum(top, jnp.max(full, axis=-1, keepdims=True))
                full = jnp.exp(full - top)
            diag = jnp.exp(diag - top)
            total = jnp.sum(diag, axis=-1, keepdims=True)
            got = dot(diag.astype(bfloat), value[start : start + rows])
            if start:
                total = total + jnp.sum(full, axis=-1, keepdims=True)
                got = got + dot(full.astype(bfloat), value[:start])
            out = jnp.where(mine, got * (1.0 / total), out)
        o_ref[start : start + rows, :] = out.astype(bfloat)


def attend_back_kernel(
    rows, q_ref, k_ref, v_ref, go_ref, keep_ref, up_ref, low_ref, out_ref, gk_ref, gv_ref
):
    pair = pl.program_id(0)
    length, lanes = q_ref.shape
    width = out_ref.shape[1] // 3
    scale = HD**-0.5
    keep, upper, lower = keep_ref[...], up_ref[...], low_ref[...]
    query = (turn(q_ref[...], keep, upper, lower).astype(bfloat).astype(single) * scale).astype(
        bfloat
    )
    key = turn(k_ref[...], keep, upper, lower).astype(bfloat)
    value = v_ref[...].astype(bfloat)
    gk_ref[...] = jnp.zeros_like(gk_ref)
    gv_ref[...] = jnp.zeros_like(gv_ref)
    lane = lax.broadcasted_iota(jnp.int32, (rows, lanes), 1) // HD
    above = lax.broadcasted_iota(jnp.int32, (rows, rows), 0) <= lax.broadcasted_iota(
        jnp.int32, (rows, rows), 1
    )
    nt = ((1,), (1,))
    tn = ((0,), (0,))
    zero = jnp.zeros((), bfloat)
    for start in range(0, length, rows):
        here = slice(start, start + rows)
        out = jnp.zeros((rows, lanes), single)
        for head in range(lanes // HD):
            mine = lane == head
            part = jnp.where(mine, query[here], zero)
            grad = jnp.where(mine, go_ref[here, :], zero)
            diag = jnp.where(above, dot(key[here], part, nt), NEG)
            top = jnp.max(diag, axis=0, keepdims=True)
            if start:
                full = dot(key[:start], part, nt)
                top = jnp.maximum(top, jnp.max(full, axis=0, keepdims=True))
                full = jnp.exp(full - top)
            diag = jnp.exp(diag - top)
            total = jnp.sum(diag, axis=0, keepdims=True)
            if start:
                total = total + jnp.sum(full, axis=0, keepdims=True)
            share = 1.0 / total
            diag = diag * share
            grad_diag = dot(value[here], grad, nt)
            delta = jnp.sum(diag * grad_diag, axis=0, keepdims=True)
            if start:
                full = full * share
                grad_full = dot(value[:start], grad, nt)
                delta = delta + jnp.sum(full * grad_full, axis=0, keepdims=True)
            score_diag = (diag * (grad_diag - delta)).astype(bfloat)
            got = dot(score_diag, key[here], tn)
            gv_ref[here, :] += dot(diag.astype(bfloat), grad)
            gk_ref[here, :] += dot(score_diag, part)
            if start:
                score_full = (full * (grad_full - delta)).astype(bfloat)
                got = got + dot(score_full, key[:start], tn)
                gv_ref[:start, :] += dot(full.astype(bfloat), grad)
                gk_ref[:start, :] += dot(score_full, part)
            out = jnp.where(mine, got * scale, out)
        out = turn_back(out.astype(bfloat).astype(single), keep[here], upper[here], lower[here])
        out_ref[here, pl.ds(pl.multiple_of(pair * lanes, lanes), lanes)] = out.astype(bfloat)
    back = turn_back(gk_ref[...].astype(bfloat).astype(single), keep, upper, lower)
    out_ref[:, pl.ds(pl.multiple_of(width + pair * lanes, lanes), lanes)] = back.astype(bfloat)
    out_ref[:, pl.ds(pl.multiple_of(2 * width + pair * lanes, lanes), lanes)] = gv_ref[
        ...
    ].astype(bfloat)


TILE = 2 * HD


def attend_whole(mixed, tables):
    length, wide = mixed.shape
    width = wide // 3
    pairs = width // TILE
    rows = min(256, length)
    table = pl.BlockSpec((length, TILE), lambda p: (0, 0))
    return pl.pallas_call(
        functools.partial(attend_kernel, rows),
        grid=(pairs,),
        in_specs=[
            pl.BlockSpec((length, TILE), lambda p: (0, p)),
            pl.BlockSpec((length, TILE), lambda p: (0, pairs + p)),
            pl.BlockSpec((length, TILE), lambda p: (0, 2 * pairs + p)),
            table,
            table,
            table,
        ],
        out_specs=pl.BlockSpec((length, TILE), lambda p: (0, p)),
        out_shape=jax.ShapeDtypeStruct((length, width), bfloat),
        cost_estimate=pl.CostEstimate(
            flops=4 * length * length * width,
            bytes_accessed=14 * length * width,
            transcendentals=length * length * width // HD,
        ),
        name="attend",
    )(mixed, mixed, mixed, *tables)


def attend_back_whole(mixed, grad_out, tables):
    length, wide = mixed.shape
    width = wide // 3
    pairs = width // TILE
    rows = min(256, length)
    table = pl.BlockSpec((length, TILE), lambda p: (0, 0))
    return pl.pallas_call(
        functools.partial(attend_back_kernel, rows),
        grid=(pairs,),
        in_specs=[
            pl.BlockSpec((length, TILE), lambda p: (0, p)),
            pl.BlockSpec((length, TILE), lambda p: (0, pairs + p)),
            pl.BlockSpec((length, TILE), lambda p: (0, 2 * pairs + p)),
            pl.BlockSpec((length, TILE), lambda p: (0, p)),
            table,
            table,
            table,
        ],
        out_specs=pl.BlockSpec((length, wide), lambda p: (0, 0)),
        out_shape=jax.ShapeDtypeStruct((length, wide), bfloat),
        scratch_shapes=[
            pltpu.VMEM((length, TILE), single),
            pltpu.VMEM((length, TILE), single),
        ],
        cost_estimate=pl.CostEstimate(
            flops=10 * length * length * width,
            bytes_accessed=20 * length * width,
            transcendentals=length * length * width // HD,
        ),
        name="attend_back",
    )(mixed, mixed, mixed, grad_out, *tables)


SWAP = [(0, 1), (1, 0)]
XPAIR = [(0, 1), (1, 0), (2, 3), (3, 2)]
YPAIR = [(0, 2), (2, 0), (1, 3), (3, 1)]
ZPAIR = [(0, 1), (1, 0), (2, 3), (3, 2)]
SPARE = 32


def over_x(value):
    return lax.ppermute(value, "fsdp", XPAIR)


def over_y(value):
    return lax.ppermute(value, "fsdp", YPAIR)


def over_core(value):
    return lax.ppermute(value, "section", SWAP)


def vmem(count):
    return [pl.BlockSpec(memory_space=pltpu.VMEM)] * count


SCALAR = pl.BlockSpec(memory_space=pltpu.SMEM)


def at_tile(index, size):
    return pl.ds(pl.multiple_of(index * size, size), size)


def pack_attn_kernel(core_ref, qkv_ref, out_ref, own_ref, send_ref):
    core = core_ref[0]
    rows, wide = own_ref.shape
    width = out_ref.shape[1] // 2
    tile = qkv_ref.shape[1] // 24
    half = out_ref.shape[0] // 2
    for which, ref in ((core, own_ref), (1 - core, send_ref)):
        for j in range(12):
            ref[:, j * tile : (j + 1) * tile] = qkv_ref[:, at_tile(2 * j + which, tile)]
        for j in range(2):
            ref[j * half : (j + 1) * half, 12 * tile :] = out_ref[
                at_tile(which, half), j * width : (j + 1) * width
            ]


def pack_mlp_kernel(core_ref, up_ref, down_ref, own_ref, send_ref):
    core = core_ref[0]
    rows = up_ref.shape[0]
    tile = up_ref.shape[1] // 8
    half = down_ref.shape[0] // 2
    for which, ref in ((core, own_ref), (1 - core, send_ref)):
        ref[:half, :] = down_ref[at_tile(which, half), :]
        for j in range(4):
            row = half + rows * (j // 2)
            ref[row : row + rows, (j % 2) * tile : (j % 2 + 1) * tile] = up_ref[
                :, at_tile(2 * j + which, tile)
            ]


def pack(kernel, shape, core, *shards):
    out = jax.ShapeDtypeStruct(shape, bfloat)
    return pl.pallas_call(
        kernel,
        in_specs=[SCALAR] + vmem(2),
        out_specs=vmem(2),
        out_shape=[out, out],
        cost_estimate=pl.CostEstimate(
            flops=0, bytes_accessed=8 * shape[0] * shape[1], transcendentals=0
        ),
        name="pack",
    )(core, *shards)


def collect(piece, line):
    rows = piece.shape[0]
    thin = rows * 5 // 16
    wide = rows - thin
    odd = line % 2
    mine = lax.dynamic_slice_in_dim(piece, odd * thin, wide, 0)
    from_x = over_x(mine)
    from_y = over_y(mine)
    corner_low = over_y(from_x[:thin])
    corner_high = over_x(from_y[thin:])
    start = odd * (wide - thin)
    share = functools.partial(lax.dynamic_slice_in_dim, slice_size=thin, axis=0)
    corner = jnp.where(odd == 0, corner_low, corner_high[wide - 2 * thin :])
    given = jnp.stack([share(from_x, start), share(from_y, start), corner])
    return piece, from_x, from_y, corner_low, corner_high, lax.ppermute(given, "seq", ZPAIR)


def place_kernel(put, where_ref, piece, from_x, from_y, low, high, given, *refs):
    whole = refs[-1]
    relative = where_ref[0] ^ pl.program_id(0)
    odd = where_ref[1]
    thin = low.shape[0]
    wide = from_x.shape[0]

    @pl.when(relative == 0)
    def _():
        whole[...] = piece[...]

    for parity in range(2):
        base = parity * thin
        other = 0 if parity else wide

        @pl.when((relative == 1) & (odd == parity))
        def _():
            whole[base : base + wide, :] = from_x[...]
            whole[other : other + thin, :] = given[0]

        @pl.when((relative == 2) & (odd == parity))
        def _():
            whole[base : base + wide, :] = from_y[...]
            whole[other : other + thin, :] = given[1]

        @pl.when((relative == 3) & (odd == parity))
        def _():
            whole[base : base + thin, :] = low[...]
            whole[base + thin : base + wide, :] = high[...]
            whole[other : other + thin, :] = given[2]

    put(whole, *refs[:-1])


def put_attn(whole, qkv_ref, out_ref):
    cut = qkv_ref.shape[1]
    half = out_ref.shape[0]
    qkv_ref[...] = whole[:, :cut]
    wide = whole.shape[1] - cut
    for j in range(2):
        out_ref[:, j * wide : (j + 1) * wide] = whole[j * half : (j + 1) * half, cut:]


def put_mlp(whole, up_ref, down_ref):
    rows = up_ref.shape[0]
    half = down_ref.shape[0]
    width = whole.shape[1]
    down_ref[...] = whole[:half, :]
    for j in range(2):
        up_ref[:, j * width : (j + 1) * width] = whole[half + j * rows : half + (j + 1) * rows, :]


def arrange(put, parts, spot, shapes):
    blocks = [(shape[0] // 4, shape[1]) for shape in shapes]
    size = parts[0].shape
    return pl.pallas_call(
        functools.partial(place_kernel, put),
        grid=(4,),
        in_specs=[SCALAR] + vmem(6),
        out_specs=[pl.BlockSpec(block, lambda i: (i, 0)) for block in blocks],
        out_shape=[jax.ShapeDtypeStruct(shape, bfloat) for shape in shapes],
        scratch_shapes=[pltpu.VMEM(size, bfloat)],
        cost_estimate=pl.CostEstimate(
            flops=0, bytes_accessed=16 * size[0] * size[1], transcendentals=0
        ),
        name="arrange",
    )(spot, *parts)


def grad_attn_kernel(a_ref, mixed_ref, att_ref, grad_ref, sums_ref, out_ref):
    rows = a_ref.shape[1]
    cut = mixed_ref.shape[1]
    half = att_ref.shape[1]
    tn = ((0,), (0,))
    out_ref[0, :rows, :cut] = dot(a_ref[...], mixed_ref[...], tn).astype(bfloat)
    got = dot(att_ref[...], grad_ref[...], tn).astype(bfloat)
    wide = got.shape[1] // 2
    out_ref[0, :half, cut:] = got[:, :wide]
    out_ref[0, half:rows, cut:] = got[:, wide:]
    sums = sums_ref[...]
    filled = jnp.concatenate(
        [sums, jnp.zeros((SPARE - sums.shape[0], sums.shape[1]), sums.dtype)], axis=0
    )
    out_ref[0, rows:, :] = jnp.zeros((SPARE, out_ref.shape[2]), bfloat)
    out_ref[0, rows:, : sums.shape[1]] = filled.astype(bfloat)


def grad_attn(normed_a, grad_mixed, attended, grad_low, sums):
    toks, width = normed_a.shape
    cut = grad_mixed.shape[1]
    half = attended.shape[1] // 4
    rows = width // 4
    wide = cut + width // 2
    return pl.pallas_call(
        grad_attn_kernel,
        grid=(4,),
        in_specs=[
            pl.BlockSpec((toks, rows), lambda i: (0, i)),
            pl.BlockSpec((toks, cut), lambda i: (0, 0)),
            pl.BlockSpec((toks, half), lambda i: (0, i)),
            pl.BlockSpec((toks, width), lambda i: (0, 0)),
            pl.BlockSpec((4, rows), lambda i: (0, i)),
        ],
        out_specs=pl.BlockSpec((1, rows + SPARE, wide), lambda i: (i, 0, 0)),
        out_shape=jax.ShapeDtypeStruct((4, rows + SPARE, wide), bfloat),
        cost_estimate=pl.CostEstimate(
            flops=2 * toks * width * wide,
            bytes_accessed=10 * toks * width,
            transcendentals=0,
        ),
        name="grad_attn",
    )(normed_a, grad_mixed, attended, grad_low, sums)


def grad_mlp_kernel(hid_ref, grad_ref, c_ref, pre_ref, out_ref):
    half = hid_ref.shape[1]
    rows = c_ref.shape[1]
    width = grad_ref.shape[1]
    tn = ((0,), (0,))
    out_ref[0, :half, :] = dot(hid_ref[...], grad_ref[...], tn).astype(bfloat)
    for j in range(2):
        out_ref[0, half + j * rows : half + (j + 1) * rows, :] = dot(
            c_ref[...], pre_ref[:, j * width : (j + 1) * width], tn
        ).astype(bfloat)


def grad_mlp(hidden, grad_low, normed_c, grad_pre):
    toks, width = grad_low.shape
    units = hidden.shape[1]
    half, rows = units // 4, width // 4
    return pl.pallas_call(
        grad_mlp_kernel,
        grid=(4,),
        in_specs=[
            pl.BlockSpec((toks, half), lambda i: (0, i)),
            pl.BlockSpec((toks, width), lambda i: (0, 0)),
            pl.BlockSpec((toks, rows), lambda i: (0, i)),
            pl.BlockSpec((toks, units), lambda i: (0, 0)),
        ],
        out_specs=pl.BlockSpec((1, half + 2 * rows, width), lambda i: (i, 0, 0)),
        out_shape=jax.ShapeDtypeStruct((4, half + 2 * rows, width), bfloat),
        cost_estimate=pl.CostEstimate(
            flops=4 * toks * width * units,
            bytes_accessed=18 * toks * width,
            transcendentals=0,
        ),
        name="grad_mlp",
    )(hidden, grad_low, normed_c, grad_pre)


def owner_block(blocks, owner, low, high):
    size = (1, high - low) + blocks.shape[2:]
    start = (owner, low) + (0,) * (blocks.ndim - 2)
    return lax.dynamic_slice(blocks, start, size)[0]


def add_low(left, right):
    return (left.astype(single) + right.astype(single)).astype(bfloat)


def reduce_plane(blocks, place):
    rows = blocks.shape[1]
    half = rows // 2
    block = functools.partial(owner_block, blocks)
    got_a = over_x(jnp.stack([block(place ^ 1, 0, half), block(place ^ 3, 0, half)]))
    got_b = over_y(jnp.stack([block(place ^ 2, half, rows), block(place ^ 3, half, rows)]))
    pass_a = over_y(add_low(block(place ^ 2, 0, half), got_a[1]))
    pass_b = over_x(add_low(block(place ^ 1, half, rows), got_b[1]))
    sum_a = block(place, 0, half).astype(single) + got_a[0].astype(single) + pass_a.astype(single)
    sum_b = block(place, half, rows).astype(single) + got_b[0].astype(single) + pass_b.astype(single)
    return sum_a.astype(bfloat), sum_b.astype(bfloat)


def reduce_line(mine, line):
    inward = lax.ppermute(mine, "seq", [(0, 1), (3, 2)])
    side = add_low(mine, inward)
    across = lax.ppermute(side, "seq", [(1, 2), (2, 1)])
    total = add_low(side, across)
    outward = lax.ppermute(total, "seq", [(1, 0), (2, 3)])
    return jnp.where((line == 0) | (line == 3), outward, total)


def layer_forward(x_low, params, tables):
    gain_one, bias_one, gain_two, bias_two, w_qkv, w_out, w_up, w_down = params
    flat = x_low.astype(single)
    mean = jnp.mean(flat, axis=-1, keepdims=True)
    cent = flat - mean
    scale = lax.rsqrt(jnp.mean(cent * cent, axis=-1, keepdims=True) + eps_norm)
    unit = cent * scale
    normed_a = (unit * gain_one + bias_one).astype(bfloat)
    normed_c = (unit * gain_two + bias_two).astype(bfloat)
    mixed = dot(normed_a, w_qkv)
    attended = attend_whole(mixed, tables)
    pre = dot(normed_c, w_up)
    phi = 0.5 * (1.0 + lax.erf(pre * (1.0 / math.sqrt(2.0))))
    hidden = (pre * phi).astype(bfloat)
    slope = (phi + pre * jnp.exp(-0.5 * pre * pre) * (1.0 / math.sqrt(2.0 * math.pi))).astype(
        bfloat
    )
    partial = (dot(attended, w_out) + dot(hidden, w_down)).astype(bfloat)
    other = over_core(partial)
    result = (flat + (partial.astype(single) + other.astype(single))).astype(bfloat)
    kept = (x_low, mean, scale, normed_a, normed_c, mixed, attended, hidden, slope)
    return result, kept


def layer_backward(grad_low, kept, params, tables, place, line):
    gain_one, bias_one, gain_two, bias_two, w_qkv, w_out, w_up, w_down = params
    x_low, mean, scale, normed_a, normed_c, mixed, attended, hidden, slope = kept
    nt = ((1,), (1,))
    grad_pre = (dot(grad_low, w_down, nt) * slope.astype(single)).astype(bfloat)
    blocks = grad_mlp(hidden, grad_low, normed_c, grad_pre)
    mlp = lax.psum_scatter(
        blocks.reshape(-1, blocks.shape[2]), "fsdp", scatter_dimension=0, tiled=True
    )
    half = mlp.shape[0] // 2
    mlp = (reduce_line(mlp[:half], line), reduce_line(mlp[half:], line))
    grad_att = dot(grad_low, w_out, nt).astype(bfloat)
    grad_mixed = attend_back_whole(mixed, grad_att, tables)
    grad_c = dot(grad_pre, w_up, nt)
    grad_a = dot(grad_mixed, w_qkv, nt)
    unit = (x_low.astype(single) - mean) * scale
    sums = jnp.stack(
        [
            jnp.sum(grad_a * unit, axis=0),
            jnp.sum(grad_a, axis=0),
            jnp.sum(grad_c * unit, axis=0),
            jnp.sum(grad_c, axis=0),
        ]
    )
    partial = (grad_a * gain_one + grad_c * gain_two).astype(bfloat)
    other = over_core(partial)
    attn = reduce_plane(grad_attn(normed_a, grad_mixed, attended, grad_low, sums), place)
    attn = tuple(reduce_line(part, line) for part in attn)
    both = partial.astype(single) + other.astype(single)
    inner = (
        both
        - jnp.mean(both, axis=-1, keepdims=True)
        - unit * jnp.mean(both * unit, axis=-1, keepdims=True)
    )
    grad_x = (grad_low.astype(single) + scale * inner).astype(bfloat)
    return grad_x, attn + mlp


def to_sequence(blocks, core):
    count, toks, width = blocks.shape
    half = toks // 2
    mine = lax.dynamic_slice_in_dim(blocks, core * half, half, 1)
    mine = lax.all_to_all(mine, "seq", split_axis=0, concat_axis=0, tiled=True)
    other = over_core(mine)
    first = jnp.where(core == 0, mine, other)
    second = jnp.where(core == 0, other, mine)
    return jnp.stack([first, second], axis=1).reshape(count * toks, width)


def from_sequence(whole, count, core, owner):
    length, width = whole.shape
    half = length // count // 2
    blocks = whole.reshape(count, 2, half, width)
    mine = lax.dynamic_index_in_dim(blocks, core, 1, keepdims=False)
    mine = lax.all_to_all(mine, "seq", split_axis=0, concat_axis=0, tiled=True)
    other = lax.ppermute(mine, "section", [(1 - owner, owner)])
    pair = (mine, other) if owner == 0 else (other, mine)
    return jnp.stack(pair, axis=1).reshape(count, 2 * half, width)


def pick_halves(core_ref, one, two, one_given, two_given, low, high):
    @pl.when(core_ref[0] == 0)
    def _():
        low[...] = one[...]
        high[...] = one_given[...]

    @pl.when(core_ref[0] != 0)
    def _():
        low[...] = two_given[...]
        high[...] = two[...]


def unpack_attn_kernel(core_ref, *refs):
    first, second = refs[0:4], refs[4:8]
    qkv_ref, out_ref, sums_ref, low, high = refs[8:]
    half = low.shape[0] // 2
    for at, group in ((0, first), (half, second)):
        pick_halves(core_ref, *group, low.at[at : at + half], high.at[at : at + half])
    rows, wide = qkv_ref.shape
    tile = wide // 24
    cut = wide // 2
    for k, part in enumerate((low, high)):
        for j in range(12):
            at = (2 * j + k) * tile
            qkv_ref[:, at : at + tile] = part[:rows, j * tile : (j + 1) * tile].astype(single)
        some = rows // 2
        width = out_ref.shape[1] // 2
        for j in range(2):
            out_ref[k * some : (k + 1) * some, j * width : (j + 1) * width] = part[
                j * some : (j + 1) * some, cut:
            ].astype(single)
    sums_ref[...] = low[rows:, :rows].astype(single) + high[rows:, :rows].astype(single)


def unpack_mlp_kernel(core_ref, *refs):
    first, second = refs[0:4], refs[4:8]
    up_ref, down_ref, low, high = refs[8:]
    half = down_ref.shape[0] // 2
    pick_halves(core_ref, *first, low, high)
    down_ref[:half, :] = low[...].astype(single)
    down_ref[half:, :] = high[...].astype(single)
    pick_halves(core_ref, *second, low, high)
    rows = up_ref.shape[0]
    tile = up_ref.shape[1] // 8
    for k, part in enumerate((low, high)):
        for j in range(4):
            at = (2 * j + k) * tile
            row = rows * (j // 2)
            up_ref[:, at : at + tile] = part[
                row : row + rows, (j % 2) * tile : (j % 2 + 1) * tile
            ].astype(single)


def unpack(kernel, core, groups, shapes, low_shape):
    flat = [part for group in groups for part in group]
    return pl.pallas_call(
        kernel,
        in_specs=[SCALAR] + vmem(8),
        out_specs=vmem(len(shapes)),
        out_shape=[jax.ShapeDtypeStruct(shape, single) for shape in shapes],
        scratch_shapes=[pltpu.VMEM(low_shape, bfloat)] * 2,
        cost_estimate=pl.CostEstimate(
            flops=0,
            bytes_accessed=sum(4 * math.prod(shape) for shape in shapes) * 3,
            transcendentals=0,
        ),
        name="unpack",
    )(core, *flat)


def on_chip(inputs, cotangent, ln1_gain, ln1_bias, ln2_gain, ln2_bias, w_qkv, w_out, w_up, w_down):
    core = lax.axis_index("section")
    line = lax.axis_index("seq")
    place = lax.axis_index("fsdp")
    core_word = core.reshape(1).astype(jnp.int32)
    spot = jnp.stack([place, line % 2]).astype(jnp.int32)
    micro, seqs, toks, width = inputs.shape
    rows = w_qkv.shape[1]
    cut = w_qkv.shape[2] // 2
    units = w_up.shape[2] // 2
    heads = width // 2
    count = micro * seqs
    attn_own, attn_send = pack(
        pack_attn_kernel, (rows, cut + heads), core_word, w_qkv[0], w_out[0]
    )
    mlp_own, mlp_send = pack(
        pack_mlp_kernel, (w_down.shape[1], width), core_word, w_up[0], w_down[0]
    )
    attn_given = over_core(attn_send)
    mlp_given = over_core(mlp_send)
    x_low = to_sequence(inputs.reshape(count, toks, width), core)
    small = jnp.stack([ln1_gain[0], ln1_bias[0], ln2_gain[0], ln2_bias[0]])
    small = lax.all_gather(small, ("section", "fsdp")).reshape(2, 4, 4, rows)
    small = small.transpose(0, 2, 1, 3).reshape(2, 4, width).astype(single)
    tables = head_tables(x_low.shape[0], TILE)
    layers = []
    for layer in range(2):
        attn = collect(jnp.where(core == layer, attn_own, attn_given), line)
        mlp = collect(jnp.where(core == layer, mlp_own, mlp_given), line)
        qkv, out = arrange(put_attn, attn, spot, ((width, cut), (heads, width)))
        up, down = arrange(put_mlp, mlp, spot, ((width, units), (units, width)))
        layers.append(tuple(small[layer]) + (qkv, out, up, down))
    mid, kept_one = layer_forward(x_low, layers[0], tables)
    last, kept_two = layer_forward(mid, layers[1], tables)
    grad_last = to_sequence(cotangent.reshape(count, toks, width), core)
    shape = (micro, seqs, toks, width)
    first = core == 0
    both = jnp.where(first, mid, last).reshape(count, toks, width)
    outputs = lax.all_to_all(both, "seq", split_axis=0, concat_axis=0, tiled=True)
    grad_mid, owned_two = layer_backward(grad_last, kept_two, layers[1], tables, place, line)
    grad_two = from_sequence(grad_mid, count, core, 1).reshape(shape)
    grad_first, owned_one = layer_backward(grad_mid, kept_one, layers[0], tables, place, line)
    grad_one = from_sequence(grad_first, count, core, 0).reshape(shape)
    input_grads = jnp.where(first, grad_one, grad_two)[None]
    groups = [
        (
            one,
            two,
            lax.ppermute(one, "section", [(1, 0)]),
            lax.ppermute(two, "section", [(0, 1)]),
        )
        for one, two in zip(owned_one, owned_two)
    ]
    grad_qkv, grad_out, sums = unpack(
        unpack_attn_kernel,
        core_word,
        groups[:2],
        (w_qkv.shape[1:], w_out.shape[1:], (SPARE, rows)),
        (rows + SPARE, cut + heads),
    )
    grad_up, grad_down = unpack(
        unpack_mlp_kernel,
        core_word,
        groups[2:],
        (w_up.shape[1:], w_down.shape[1:]),
        (w_down.shape[1] // 2, width),
    )
    norms = tuple(sums[index : index + 1] for index in range(4))
    large = tuple(part[None] for part in (grad_qkv, grad_out, grad_up, grad_down))
    return (outputs.reshape((1,) + shape), input_grads) + norms + large


def on_any(inputs, *rest):
    micro, seqs, toks, _ = inputs.shape
    sizes = (lax.axis_size("section"), lax.axis_size("seq"), lax.axis_size("fsdp"))
    if sizes == (2, 4, 4) and micro * seqs == 4 and toks % 64 == 0:
        return on_chip(inputs, *rest)
    return on_device(inputs, *rest)


def solution(mesh):
    in_specs = (
        P(None, "fsdp", "seq", None),
        P(None, "fsdp", "seq", None),
        P("section", "fsdp"),
        P("section", "fsdp"),
        P("section", "fsdp"),
        P("section", "fsdp"),
        P("section", "fsdp", None),
        P("section", "fsdp", None),
        P("section", "fsdp", None),
        P("section", "fsdp", None),
    )
    out_specs = (
        P("section", None, "fsdp", "seq", None),
        P("section", None, "fsdp", "seq", None),
        P("section", "fsdp"),
        P("section", "fsdp"),
        P("section", "fsdp"),
        P("section", "fsdp"),
        P("section", "fsdp", None),
        P("section", "fsdp", None),
        P("section", "fsdp", None),
        P("section", "fsdp", None),
    )
    return jax.shard_map(
        on_any, mesh=mesh, in_specs=in_specs, out_specs=out_specs, check_vma=False
    )
```
